256 devices in a mesh: row: 8 (over z_lo, y), col: 32 (over x, z_hi, core).
Axes of the slice: x: 4, y: 4, z: 8 (z_hi: 4, z_lo: 2; z = z_hi * 2 + z_lo), core: 2. Of those that a mesh axis runs over, the one named last changes fastest.
Arguments:
- head_rows: float32 [262144, 256], P(('row', 'col')), may hold values from -5 to 5
- head_state: float32 [262144], P(('row', 'col')), may hold values from 0.01 to 1
- tail_rows: float32 [262144, 256], P(('row', 'col')), may hold values from -60 to 60
- tail_state: float32 [262144], P(('row', 'col')), may hold values from 0.01 to 1
- relation: float32 [8, 256, 256], replicated, may hold values from -1.5 to 1.5
- relation_state: float32 [8, 256], replicated, may hold values from 0.01 to 1
- edge_head: int32 [2, 262144], P(None, ('row', 'col')), may hold values from 0 to 1023
- edge_tail: int32 [2, 262144], P(None, ('row', 'col')), may hold values from 0 to 1023
Outputs:
- head_out: float32 [262144, 256], P(('row', 'col'))
- head_state_out: float32 [262144], P(('row', 'col'))
- tail_out: float32 [262144, 256], P(('row', 'col'))
- tail_state_out: float32 [262144], P(('row', 'col'))
- relation_out: float32 [8, 256, 256], replicated
- relation_state_out: float32 [8, 256], replicated
The draws below stay inside these ranges and needn't reach their ends.
Inputs may be any that keep to these rules, and one draw needn't show every extreme that they name: `edge_head`: a head row of the device's own block. `edge_tail`: a tail row of the block the device holds in that round.
All inputs are finite; a program needn't handle non-finite values.
Results may differ from the reference program's by a relative error of at most 0.0003.
Values sent between devices are 32-bit elements; how exact they have to be, the bound alone decides.
No kernel may reach another device: no remote copies, remote signals or barrier semaphores. Data moves between devices by JAX's collectives and lax.ppermute only.
A program may use at most 64 MiB of HBM per device.

```python
import math
import jax
import jax.numpy as jnp
from jax import lax

D = 256
R = 8
H_DEV = 1024
T_DEV = 1024
E_DEV = 1024
ROUNDS = 2
HEADS_ALL = 262144
TAILS_ALL = 262144
EDGES_ALL = 262144
N_ROW = 8
N_COL = 32
DEVICES = 256


def draw_tail_rows(key, part):
    first = jax.random.fold_in(key, 0)
    values = 0.35 * jax.random.normal(first, (TAILS_ALL, D), jnp.float32)
    values = jnp.clip(values, -2.0, 2.0)
    return values


def touch_ends(values, key, least, largest):
    longest = values.shape.index(max(values.shape))
    spots = []
    for shift in (0, 1):
        where = [jax.random.randint(jax.random.fold_in(key, axis), (), 0, length) for axis, length in enumerate(values.shape)]
        where[longest] = (where[longest] + shift) % values.shape[longest]
        spots.append(tuple(where))
    return values.at[spots[0]].set(least).at[spots[1]].set(largest)


def block_scale(rng, shape, pieces, least, high):
    factor_of = 1.0
    for dim, parts in pieces:
        draws = jax.random.uniform(jax.random.fold_in(jax.random.fold_in(rng, 6), dim), (parts,), jnp.float32, least / len(pieces), high / len(pieces))
        factor_of = factor_of * jnp.repeat(jnp.exp(draws), shape[dim] // parts).reshape((-1,) + (1,) * (len(shape) - 1 - dim))
    return factor_of


def gaussian(stream_key, dims, width, bound, cuts=(), kind=jnp.bfloat16):
    values = jax.random.normal(stream_key, dims, jnp.float32) * width
    if len(cuts) > 0:
        values = block_scale(stream_key, dims, cuts, -0.22, 0.18) * values
    return jnp.clip(values, min=-bound, max=bound).astype(kind)


def setup_inputs(seed: int = 0) -> dict:
    splits = jax.random.split(jax.random.key(seed), 9)
    return {
        "head_rows": gaussian(splits[0], (HEADS_ALL, D), 0.35, 5.0, ((0, 256),), jnp.float32),
        "head_state": jnp.clip(jnp.exp(math.log(1.0) - 4.6051702 * jax.random.uniform(splits[1], (HEADS_ALL,), jnp.float32) ** block_scale(splits[1], (HEADS_ALL,), ((0, 256),), -0.2, 0.2)), 0.01, 1.0),
        "tail_rows": draw_tail_rows(jax.random.fold_in(splits[8], 71), 0),
        "tail_state": jnp.clip(jnp.exp(math.log(1.0) - 4.6051702 * jax.random.uniform(splits[3], (TAILS_ALL,), jnp.float32) ** block_scale(splits[3], (TAILS_ALL,), ((0, 256),), -0.2, 0.2)), 0.01, 1.0),
        "relation": gaussian(splits[4], (R, D, D), 0.1, 1.5, (), jnp.float32),
        "relation_state": jnp.clip(jnp.exp(jax.random.uniform(splits[5], (R, D), jnp.float32, math.log(0.01), math.log(1.0))), 0.01, 1.0),
        "edge_head": touch_ends(jax.random.randint(splits[6], (ROUNDS, EDGES_ALL), 0, H_DEV), jax.random.fold_in(splits[6], 1), 0, H_DEV - 1).astype(jnp.int32),
        "edge_tail": touch_ends(jax.random.randint(splits[7], (ROUNDS, EDGES_ALL), 0, T_DEV), jax.random.fold_in(splits[7], 1), 0, T_DEV - 1).astype(jnp.int32),
    }


HIGHEST = lax.Precision.HIGHEST
LEARN_RATE = 0.1
RELATION_RATE = 0.1

def adagrad(values, accumulator, gradient, step_rate):
    accumulator = accumulator + lax.optimization_barrier(jnp.mean(gradient * gradient, axis=-1))
    return (values - step_rate * gradient / jnp.sqrt(accumulator)[..., None], accumulator)

def edge_bucket(head_rows, head_state, tail_rows, tail_state, relation, edge_head, edge_tail):
    rel_count = relation.shape[0]
    picked = head_rows[edge_head]
    grouped = picked.reshape(rel_count, -1, picked.shape[1])
    query = jnp.einsum('rnd,rde->rne', grouped, relation, precision=HIGHEST).reshape(picked.shape)
    scores = jnp.einsum('ed,td->et', query, tail_rows, precision=HIGHEST)
    row_max = lax.optimization_barrier(jnp.max(scores, axis=1, keepdims=True))
    exp_scores = jnp.exp(scores - row_max)
    weights = exp_scores / lax.optimization_barrier(jnp.sum(exp_scores, axis=1, keepdims=True))
    target = (edge_tail[:, None] == jnp.arange(tail_rows.shape[0], dtype=jnp.int32)[None, :]).astype(jnp.float32)
    residue = weights - target
    grad_query = jnp.dot(residue, tail_rows, precision=HIGHEST)
    grad_tail = jnp.einsum('et,ed->td', residue, query, precision=HIGHEST)
    query_groups = grad_query.reshape(grouped.shape)
    grad_picked = jnp.einsum('rne,rde->rnd', query_groups, relation, precision=HIGHEST).reshape(picked.shape)
    grad_rel = jnp.einsum('rnd,rne->rde', grouped, query_groups, precision=HIGHEST)
    grad_head = jax.ops.segment_sum(grad_picked, edge_head, num_segments=head_rows.shape[0])
    head_rows, head_state = adagrad(head_rows, head_state, grad_head, LEARN_RATE)
    tail_rows, tail_state = adagrad(tail_rows, tail_state, grad_tail, LEARN_RATE)
    return (head_rows, head_state, tail_rows, tail_state, grad_rel)

def exchange_blocks(array):
    shaped = array.reshape(N_ROW, 2, N_COL // 2, -1)
    shaped = jnp.flip(shaped, axis=1)
    return shaped.reshape(array.shape)

def reference(head_rows, head_state, tail_rows, tail_state, relation, relation_state, edge_head, edge_tail):
    total = jnp.zeros(relation.shape, jnp.float32)
    for current in range(ROUNDS):

        def device_step(running, device_entry):
            head_block_rows, head_block_state, tail_block_rows, tail_block_state, block_edge_heads, block_edge_tails = device_entry
            final_output = edge_bucket(head_block_rows, head_block_state, tail_block_rows, tail_block_state, relation, block_edge_heads, block_edge_tails)
            return (running + final_output[4], final_output[:4])
        items = (head_rows.reshape(DEVICES, H_DEV, D), head_state.reshape(DEVICES, H_DEV), tail_rows.reshape(DEVICES, T_DEV, D), tail_state.reshape(DEVICES, T_DEV), edge_head[current].reshape(DEVICES, E_DEV), edge_tail[current].reshape(DEVICES, E_DEV))
        total, outputs = lax.scan(device_step, total, items)
        head_rows = outputs[0].reshape(HEADS_ALL, D)
        head_state = outputs[1].reshape(HEADS_ALL)
        tail_rows = outputs[2].reshape(TAILS_ALL, D)
        tail_state = outputs[3].reshape(TAILS_ALL)
        if current + 1 < ROUNDS:
            tail_rows = exchange_blocks(tail_rows)
            tail_state = exchange_blocks(tail_state)
    relation, relation_state = adagrad(relation, relation_state, total, RELATION_RATE)
    return (head_rows, head_state, tail_rows, tail_state, relation, relation_state)
```

```python
import jax
import jax.numpy as jnp
from jax import lax
from jax.sharding import Mesh, PartitionSpec as P

HIGHEST = lax.Precision.HIGHEST
LEARN_RATE = 0.1
RELATION_RATE = 0.1
AXES = ("zl", "y", "x", "zh", "core")
PLANE = ("y", "x")
LINE = ("zl", "zh")
barrier = lax.optimization_barrier


def exchanged(x, axis, stride):
    return lax.ppermute(x, axis, [(i, i ^ stride) for i in range(lax.axis_size(axis))])


def adagrad(values, accumulator, gradient, step_rate):
    accumulator = accumulator + jnp.mean(gradient * gradient, axis=-1)
    return (values - step_rate * gradient / jnp.sqrt(accumulator)[..., None], accumulator)


def edge_bucket(head_rows, head_state, tail_rows, tail_state, relation, edge_head, edge_tail):
    rel_count = relation.shape[0]
    picked = head_rows[edge_head]
    grouped = picked.reshape(rel_count, -1, picked.shape[1])
    query = jnp.einsum("rnd,rde->rne", grouped, relation, precision=HIGHEST).reshape(picked.shape)
    scores = jnp.einsum("ed,td->et", query, tail_rows, precision=HIGHEST)
    row_max = jnp.max(scores, axis=1, keepdims=True)
    exp_scores = jnp.exp(scores - row_max)
    weights = exp_scores / jnp.sum(exp_scores, axis=1, keepdims=True)
    target = (
        edge_tail[:, None] == jnp.arange(tail_rows.shape[0], dtype=jnp.int32)[None, :]
    ).astype(jnp.float32)
    residue = weights - target
    grad_query = jnp.dot(residue, tail_rows, precision=HIGHEST)
    grad_tail = jnp.einsum("et,ed->td", residue, query, precision=HIGHEST)
    query_groups = grad_query.reshape(grouped.shape)
    grad_picked = jnp.einsum("rne,rde->rnd", query_groups, relation, precision=HIGHEST).reshape(
        picked.shape
    )
    grad_rel = jnp.einsum("rnd,rne->rde", grouped, query_groups, precision=HIGHEST)
    grad_head = jax.ops.segment_sum(grad_picked, edge_head, num_segments=head_rows.shape[0])
    head_rows, head_state = adagrad(head_rows, head_state, grad_head, LEARN_RATE)
    tail_rows, tail_state = adagrad(tail_rows, tail_state, grad_tail, LEARN_RATE)
    return (head_rows, head_state, tail_rows, tail_state, grad_rel)


def scattered(x, axes):
    count = lax.axis_size(axes)
    parts = x.reshape(count, -1, x.shape[1])
    parts = lax.all_to_all(parts, axes, 0, 0, tiled=True)
    return jnp.sum(parts, axis=0)


def gathered(x, axes):
    count = lax.axis_size(axes)
    parts = jnp.broadcast_to(x[None], (count,) + x.shape)
    parts = lax.all_to_all(parts, axes, 0, 0, tiled=True)
    return parts.reshape(-1, x.shape[1])


def summed(total):
    flat = total.reshape(-1, total.shape[-1])
    half = flat.shape[0] // 2
    core = lax.axis_index("core")
    kept = lax.dynamic_slice_in_dim(flat, core * half, half, 0)
    sent = lax.dynamic_slice_in_dim(flat, (1 - core) * half, half, 0)
    piece = kept + exchanged(sent, "core", 1)
    piece = scattered(piece, PLANE)
    piece = scattered(piece, LINE)
    piece = gathered(piece, LINE)
    piece = gathered(piece, PLANE)
    other = exchanged(piece, "core", 1)
    low = jnp.where(core == 0, piece, other)
    high = jnp.where(core == 0, other, piece)
    return jnp.concatenate([low, high], axis=0).reshape(total.shape)


def shards(
    head_rows, head_state, tail_rows, tail_state, relation, relation_state, edge_head, edge_tail
):
    rounds = edge_head.shape[0]
    total = jnp.zeros(relation.shape, jnp.float32)
    for current in range(rounds):
        head_rows, head_state, tail_rows, tail_state, grad_rel = edge_bucket(
            head_rows,
            head_state,
            tail_rows,
            tail_state,
            relation,
            edge_head[current],
            edge_tail[current],
        )
        total = total + grad_rel
        if current + 1 < rounds:
            tail_rows, tail_state = exchanged((tail_rows, tail_state), "x", 2)
    summed_rel = summed(total)
    relation, relation_state = adagrad(relation, relation_state, summed_rel, RELATION_RATE)
    return (head_rows, head_state, tail_rows, tail_state, relation, relation_state)


def solution(mesh):
    fine = Mesh(mesh.devices.reshape(2, 4, 4, 4, 2), AXES)
    in_specs = (
        P(AXES, None),
        P(AXES),
        P(AXES, None),
        P(AXES),
        P(),
        P(),
        P(None, AXES),
        P(None, AXES),
    )
    out_specs = (
        P(AXES, None),
        P(AXES),
        P(AXES, None),
        P(AXES),
        P(),
        P(),
    )
    return jax.shard_map(shards, mesh=fine, in_specs=in_specs, out_specs=out_specs, check_vma=False)
```

```python
import jax
import jax.numpy as jnp
from jax import lax
from jax.experimental import pallas as pl
from jax.experimental.pallas import tpu as pltpu
from jax.sharding import Mesh, PartitionSpec as P

LEARN_RATE = 0.1
RELATION_RATE = 0.1
AXES = ("zl", "y", "x", "zh", "core")
CUBE = ("zl", "y", "x")
LINE = ("zh",)
TILE = 256
F32 = jnp.float32
BF16 = jnp.bfloat16
NN = (((1,), (0,)), ((), ()))
NT = (((1,), (1,)), ((), ()))


def mul(a, b, dims):
    return lax.dot_general(a, b, dims, preferred_element_type=F32)


def parts(x, count):
    found = []
    for _ in range(count):
        part = x.astype(BF16)
        found.append(part)
        x = x - part.astype(F32)
    return found


def product6(a, b, dims):
    a1, a2, a3 = a
    b1, b2, b3 = b
    small = mul(a1, b3, dims) + mul(a3, b1, dims) + mul(a2, b2, dims)
    return mul(a1, b1, dims) + (mul(a1, b2, dims) + mul(a2, b1, dims) + small)


def product3(a, b, dims):
    return mul(a[0], b[0], dims) + (mul(a[0], b[1], dims) + mul(a[1], b[0], dims))


def column(row):
    return jnp.broadcast_to(row, (128, row.shape[1])).T


def equal_lanes(col, width):
    lanes = lax.broadcasted_iota(jnp.int32, (col.shape[0], width), 1).astype(F32)
    return col[:, :1] == lanes


def tile_of(i):
    return pl.ds(pl.multiple_of(i * TILE, TILE), TILE)


def store_parts(source, refs):
    for ref, part in zip(refs, parts(source, len(refs))):
        ref[...] = part


def picked_query(i, col, head_parts, rel_ref, picked_ref, query_ref):
    rows = tile_of(i)
    hot = jnp.where(equal_lanes(col[rows, :], head_parts[0].shape[0]), 1.0, 0.0).astype(BF16)
    p1, p2, p3 = (mul(hot, ref[...], NN) for ref in head_parts)
    picked = p1 + (p2 + p3)
    picked_ref[rows, :] = picked
    groups = []
    width = picked.shape[0] // 2
    for j in range(2):
        rel = parts(rel_ref[2 * i + j], 3)
        mine = parts(picked[j * width : (j + 1) * width], 3)
        groups.append(product6(mine, rel, NN))
    query_ref[rows, :] = jnp.concatenate(groups, axis=0)


def residue_of(i, query, tail_parts, target_col, r1_ref, r2_ref):
    rows = tile_of(i)
    scores = product6(parts(query, 3), [ref[...] for ref in tail_parts], NT)
    peak = jnp.max(scores, axis=1, keepdims=True)
    powers = jnp.exp(scores - peak)
    weights = powers * (1.0 / jnp.sum(powers, axis=1, keepdims=True))
    hit = equal_lanes(target_col[rows, :], scores.shape[1])
    residue = jnp.where(hit, weights - 1.0, weights)
    r1, r2 = parts(residue, 2)
    r1_ref[rows, :] = r1
    r2_ref[rows, :] = r2
    return r1, r2


def updated(gradient_t, state, rate):
    width = gradient_t.shape[0]
    state = state + jnp.sum(gradient_t * gradient_t, axis=0, keepdims=True) * (1.0 / width)
    return state, (gradient_t * (rate / jnp.sqrt(state))).T


def loop(count, body):
    def step(i, carry):
        body(i)
        return carry

    lax.fori_loop(0, count, step, 0)


def first_kernel(
    head_ref, tail_ref, state_ref, rel_ref, eh_ref, et_ref,
    new_tail, new_state, r1_ref, r2_ref, picked_ref,
    query_ref, h1, h2, h3, t1, t2, t3, head_col, tail_col, grad,
):
    store_parts(head_ref[...], (h1, h2, h3))
    store_parts(tail_ref[...], (t1, t2, t3))
    head_col[...] = column(eh_ref[0:1, :].astype(F32))
    tail_col[...] = column(et_ref[0:1, :].astype(F32))
    grad[...] = jnp.zeros_like(grad)

    def body(i):
        picked_query(i, head_col, (h1, h2, h3), rel_ref, picked_ref, query_ref)
        query = query_ref[tile_of(i), :]
        residue = residue_of(i, query, (t1, t2, t3), tail_col, r1_ref, r2_ref)
        grad[...] += product3(parts(query.T, 2), residue, NN)

    loop(head_ref.shape[0] // TILE, body)
    state, step = updated(grad[...], state_ref[...], LEARN_RATE)
    new_state[...] = state
    new_tail[...] = tail_ref[...] - step


def head_update(i, query_grad, rel_ref, col, grad, each):
    rows = tile_of(i)
    width = TILE // 2
    groups = []
    for j in range(2):
        mine = query_grad[j * width : (j + 1) * width]
        pair = parts(mine, 2)
        groups.append(product3(pair, parts(rel_ref[2 * i + j], 2), NT))
        if each is not None:
            each(2 * i + j, pair)
    g1, g2 = parts(jnp.concatenate(groups, axis=0).T, 2)
    hot = jnp.where(equal_lanes(col[rows, :], grad.shape[1]), 1.0, 0.0).astype(BF16)
    grad[...] += mul(g1, hot, NN) + mul(g2, hot, NN)


def relation_grad(picked_ref, group, pair):
    width = TILE // 2
    rows = pl.ds(pl.multiple_of(group * width, width), width)
    return product3(parts(picked_ref[rows, :].T, 2), pair, NN)


def second_kernel(
    r1_ref, r2_ref, tail_ref, picked_ref, rel_ref, head_ref, state_ref, eh_ref,
    new_head, new_state, rel_grad, picked_next, query_next,
    t1, t2, h1, h2, h3, col, next_col, grad,
):
    store_parts(tail_ref[...], (t1, t2))
    col[...] = column(eh_ref[0:1, :].astype(F32))
    next_col[...] = column(eh_ref[1:2, :].astype(F32))
    grad[...] = jnp.zeros_like(grad)

    def body(i):
        rows = tile_of(i)
        query_grad = product3((r1_ref[rows, :], r2_ref[rows, :]), (t1[...], t2[...]), NN)

        def each(group, pair):
            rel_grad[group] = relation_grad(picked_ref, group, pair)

        head_update(i, query_grad, rel_ref, col, grad, each)

    count = head_ref.shape[0] // TILE
    loop(count, body)
    state, step = updated(grad[...], state_ref[...], LEARN_RATE)
    new_state[...] = state
    moved = head_ref[...] - step
    new_head[...] = moved
    store_parts(moved, (h1, h2, h3))
    loop(
        count,
        lambda i: picked_query(i, next_col, (h1, h2, h3), rel_ref, picked_next, query_next),
    )


def third_kernel(
    query_ref, tail_ref, picked_ref, rel_grad_ref, et_ref,
    rel_grad, query_grad_ref, r1_ref, r2_ref,
    t1, t2, t3, tail_col,
):
    store_parts(tail_ref[...], (t1, t2, t3))
    tail_col[...] = column(et_ref[1:2, :].astype(F32))

    def body(i):
        rows = tile_of(i)
        residue = residue_of(i, query_ref[rows, :], (t1, t2, t3), tail_col, r1_ref, r2_ref)
        query_grad = product3(residue, (t1[...], t2[...]), NN)
        query_grad_ref[rows, :] = query_grad
        width = TILE // 2
        for j in range(2):
            group = 2 * i + j
            pair = parts(query_grad[j * width : (j + 1) * width], 2)
            rel_grad[group] = rel_grad_ref[group] + relation_grad(picked_ref, group, pair)

    loop(query_ref.shape[0] // TILE, body)


def tail_kernel(query_ref, r1_ref, r2_ref, tail_ref, state_ref, new_tail, new_state, grad):
    grad[...] = jnp.zeros_like(grad)

    def body(i):
        rows = tile_of(i)
        turned = parts(query_ref[rows, :].T, 2)
        grad[...] += product3(turned, (r1_ref[rows, :], r2_ref[rows, :]), NN)

    loop(query_ref.shape[0] // TILE, body)
    state, step = updated(grad[...], state_ref[...], LEARN_RATE)
    new_state[...] = state
    new_tail[...] = tail_ref[...] - step


def head_kernel(query_grad_ref, rel_ref, head_ref, state_ref, eh_ref, new_head, new_state, col, grad):
    col[...] = column(eh_ref[1:2, :].astype(F32))
    grad[...] = jnp.zeros_like(grad)
    loop(
        head_ref.shape[0] // TILE,
        lambda i: head_update(i, query_grad_ref[tile_of(i), :], rel_ref, col, grad, None),
    )
    state, step = updated(grad[...], state_ref[...], LEARN_RATE)
    new_state[...] = state
    new_head[...] = head_ref[...] - step


def relation_kernel(mine_ref, other_ref, core_ref, rel_ref, state_ref, new_rel, new_state):
    core = core_ref[0]
    half = mine_ref.shape[0]
    size = rel_ref.shape[1]

    def update(group, gradient):
        mean = jnp.sum(gradient * gradient, axis=1, keepdims=True) * (1.0 / size)
        state = column(state_ref[pl.ds(group, 1), :]) + mean
        new_state[pl.ds(group, 1), :] = state.T[0:1, :]
        new_rel[group] = rel_ref[group] - gradient * (RELATION_RATE / jnp.sqrt(state[:, :1]))

    def body(i):
        update(core * half + i, mine_ref[i])
        update((1 - core) * half + i, other_ref[i])

    loop(half, body)


def call(kernel, outs, scratch, flops, *args, smem=()):
    vmem = pl.BlockSpec(memory_space=pltpu.VMEM)
    specs = [pl.BlockSpec(memory_space=pltpu.SMEM) if k in smem else vmem for k in range(len(args))]
    moved = sum(a.size * a.dtype.itemsize for a in (*args, *outs))
    return pl.pallas_call(
        kernel,
        out_shape=outs,
        in_specs=specs,
        out_specs=[vmem] * len(outs),
        scratch_shapes=scratch,
        compiler_params=pltpu.CompilerParams(vmem_limit_bytes=36 << 20),
        cost_estimate=pl.CostEstimate(flops=flops, bytes_accessed=moved, transcendentals=0),
        name=kernel.__name__,
    )(*args)


def exchanged(x, axis, stride):
    return lax.ppermute(x, axis, [(i, i ^ stride) for i in range(lax.axis_size(axis))])


def spread(x, axes):
    blocks = jnp.broadcast_to(x[None], (lax.axis_size(axes),) + x.shape)
    return lax.all_to_all(blocks, axes, 0, 0, tiled=True)


def summed_half(total):
    half, rows, width = total.shape[0] // 2, total.shape[1], total.shape[2]
    core = lax.axis_index("core")
    kept = lax.dynamic_slice_in_dim(total, core * half, half, 0)
    sent = lax.dynamic_slice_in_dim(total, (1 - core) * half, half, 0)
    piece = (kept + exchanged(sent, "core", 1)).reshape(lax.axis_size(CUBE), -1, width)
    piece = jnp.sum(lax.all_to_all(piece, CUBE, 0, 0, tiled=True), axis=0)
    piece = jnp.sum(spread(piece, LINE), axis=0)
    return spread(piece, CUBE).reshape(half, rows, width)


def like(*shape, dtype=F32):
    return jax.ShapeDtypeStruct(shape, dtype)


def shards(
    head_rows, head_state, tail_rows, tail_state, relation, relation_state, edge_head, edge_tail
):
    heads, width = head_rows.shape
    tails = tail_rows.shape[0]
    edges = edge_head.shape[1]
    unit = 2 * edges * width * tails
    state_shape = (1, heads)
    hs = head_state.reshape(state_shape)
    ts = tail_state.reshape(state_shape)
    entity = like(heads, width)
    srow = like(*state_shape)
    wide = like(edges, tails, dtype=BF16)
    bank = pltpu.VMEM((heads, width), BF16)
    cols = pltpu.VMEM((edges, 128), F32)
    grad = pltpu.VMEM((width, heads), F32)

    tail1, ts1, r1, r2, picked = call(
        first_kernel,
        (entity, srow, wide, wide, entity),
        [pltpu.VMEM((edges, width), F32)] + [bank] * 6 + [cols] * 2 + [grad],
        unit * 14,
        head_rows, tail_rows, ts, relation, edge_head, edge_tail,
    )
    tail_in, ts_in = exchanged((tail1, ts1), "x", 2)
    head1, hs1, rel_grad, picked2, query2 = call(
        second_kernel,
        (entity, srow, like(*relation.shape), entity, entity),
        [bank] * 5 + [cols] * 2 + [grad],
        unit * 11,
        r1, r2, tail_rows, picked, relation, head_rows, hs, edge_head,
    )
    total, query_grad, r1, r2 = call(
        third_kernel,
        (like(*relation.shape), entity, wide, wide),
        [bank] * 3 + [cols],
        unit * 10,
        query2, tail_in, picked2, rel_grad, edge_tail,
    )
    mine = summed_half(total)
    tail2, ts2 = call(
        tail_kernel, (entity, srow), [grad], unit * 3, query2, r1, r2, tail_in, ts_in
    )
    head2, hs2 = call(
        head_kernel, (entity, srow), [cols, grad], unit * 3,
        query_grad, relation, head1, hs1, edge_head,
    )
    other = exchanged(mine, "core", 1)
    core = lax.axis_index("core").astype(jnp.int32).reshape(1)
    relation, relation_state = call(
        relation_kernel,
        (like(*relation.shape), like(*relation_state.shape)),
        [],
        8 * relation.size,
        mine, other, core, relation, relation_state,
        smem=(2,),
    )
    return (
        head2,
        hs2.reshape(heads),
        tail2,
        ts2.reshape(tails),
        relation,
        relation_state,
    )


def solution(mesh):
    fine = Mesh(mesh.devices.reshape(2, 4, 4, 4, 2), AXES)
    in_specs = (
        P(AXES, None),
        P(AXES),
        P(AXES, None),
        P(AXES),
        P(),
        P(),
        P(None, AXES),
        P(None, AXES),
    )
    out_specs = (
        P(AXES, None),
        P(AXES),
        P(AXES, None),
        P(AXES),
        P(),
        P(),
    )
    return jax.shard_map(shards, mesh=fine, in_specs=in_specs, out_specs=out_specs, check_vma=False)
```
